32 devices in a mesh: row: 4 (over y, x), col: 8 (over z, core).
Axes of the slice: x: 2, y: 2, z: 4, core: 2. Of those that a mesh axis runs over, the one named last changes fastest.
Arguments:
- loads: float32 [4, 8, 1024, 8], P('row', 'col'), may hold values from -6 to 6
- schur: float32 [4, 8, 1024, 1024], P('row', 'col'), may hold values from -0.5 to 4.5, as said below
- factor: float32 [4, 8, 1024, 1024], P('row', 'col'), may hold values from -0.5 to 0.6, as said below
- coarse_inverse: float32 [1536, 1536], P(('row', 'col')), may hold values from -0.5 to 1.5, as said below
- elements: int32 [4, 8], P('row', 'col'), may hold values from 4096 to 16383
- west_map: int32 [4, 8, 256], P('row', 'col'), may hold values from 0 to 255, each once within a row
- south_map: int32 [4, 8, 256], P('row', 'col'), may hold values from 0 to 255, each once within a row
- prim_local: int32 [4, 8, 48], P('row', 'col'), may hold values from 0 to 1023
- prim_coarse: int32 [4, 8, 48], P('row', 'col'), may hold values from 0 to 1535
Outputs:
- solution: float32 [4, 8, 1024, 8], P('row', 'col')
- residual: float32 [4, 8, 1024, 8], P('row', 'col')
The draws below stay inside these ranges and needn't reach their ends.
Inputs may be any that keep to these rules, and one draw needn't show every extreme that they name: `schur`: symmetric positive definite. `factor`: symmetric positive definite. `coarse_inverse`: symmetric positive definite. `west_map`: each subdomain's row is a permutation of 0 to 255. `south_map`: each subdomain's row is a permutation of 0 to 255. `prim_local`: values may repeat. `prim_coarse`: values may repeat, within a subdomain and between subdomains.
All inputs are finite; a program needn't handle non-finite values.
Results may differ from the reference program's by a relative error of at most 0.0001.
Values sent between devices are 32-bit elements; how exact they have to be, the bound alone decides.
A program may use at most 128 MiB of HBM per device.

```python
import math
import jax
import jax.numpy as jnp
from jax import lax

NI = 1024
NPRIM = 48
NRHS = 8
ITERS = 1
ELEM_BASE = 4096
FACE = 256
NCO = 1536
N_ROW = 4
N_COL = 8


def symmetric_noise(key, leading, order):
    shape = leading + (order, order)
    base = jnp.clip(jax.random.normal(key, shape, jnp.float32), -6.0, 6.0)
    return (base + jnp.swapaxes(base, -1, -2)) / math.sqrt(2.0)


def schur_diagonal(key):
    spread = jax.random.uniform(jax.random.fold_in(key, 3), (N_ROW, N_COL, NI), jnp.float32)
    return 2.0 * jnp.exp(spread * math.log(2.0))


def draw_schur(key, part):
    diagonal = schur_diagonal(key)
    noise = symmetric_noise(jax.random.fold_in(key, 7), (N_ROW, N_COL), NI)
    return diagonal[..., None] * jnp.eye(NI, dtype=jnp.float32) + 0.5 / math.sqrt(NI) * noise


def draw_factor(key, part):
    diagonal = schur_diagonal(key)
    noise = symmetric_noise(jax.random.fold_in(key, 9), (N_ROW, N_COL), NI)
    return (1.0 / diagonal)[..., None] * jnp.eye(NI, dtype=jnp.float32) + 0.04 / math.sqrt(NI) * noise


def draw_coarse_inverse(key, part):
    diagonal = 0.5 + 0.5 * jax.random.uniform(jax.random.fold_in(key, 5), (NCO,), jnp.float32)
    noise = symmetric_noise(jax.random.fold_in(key, 13), (), NCO)
    return diagonal[:, None] * jnp.eye(NCO, dtype=jnp.float32) + 0.15 / math.sqrt(NCO) * noise


def with_ends(values, rng, smallest, high):
    longest = values.shape.index(max(values.shape))
    spots = []
    for shift in (0, 1):
        where = [jax.random.randint(jax.random.fold_in(rng, axis), (), 0, length) for axis, length in enumerate(values.shape)]
        where[longest] = (where[longest] + shift) % values.shape[longest]
        spots.append(tuple(where))
    return values.at[spots[0]].set(smallest).at[spots[1]].set(high)


def steps_of(own_key, shape, pieces, low, high):
    gain, own = 1.0, jax.random.fold_in(own_key, 6)
    for position, shards_of in pieces:
        draws = jnp.exp(jax.random.uniform(jax.random.fold_in(own, position), (shards_of,), jnp.float32, low / len(pieces), high / len(pieces)))
        gain = gain * jnp.repeat(draws, shape[position] // shards_of).reshape([-1 if axis == position else 1 for axis in range(len(shape))])
    return gain


def gaussian(rng, dims, scale, limit, pieces=(), held_as=jnp.bfloat16):
    values = scale * jax.random.normal(rng, dims, jnp.float32)
    if pieces:
        values = values * steps_of(rng, dims, pieces, -0.22, 0.18)
    return jnp.clip(values, -limit, limit).astype(held_as)


def setup_inputs(seed: int = 0) -> dict:
    seeds = jax.random.split(jax.random.key(seed), 10)
    return {
        "loads": gaussian(seeds[0], (N_ROW, N_COL, NI, NRHS), 1.0, 6.0, ((0, 4), (1, 8)), jnp.float32),
        "schur": draw_schur(jax.random.fold_in(seeds[9], 71), 0),
        "factor": draw_factor(jax.random.fold_in(seeds[9], 71), 0),
        "coarse_inverse": draw_coarse_inverse(jax.random.fold_in(seeds[9], 71), 0),
        "elements": with_ends(jax.random.randint(seeds[4], (N_ROW, N_COL), ELEM_BASE, 4 * ELEM_BASE), jax.random.fold_in(seeds[4], 1), ELEM_BASE, (4 * ELEM_BASE) - 1).astype(jnp.int32),
        "west_map": jax.vmap(lambda own: jax.random.permutation(own, FACE))(jax.random.split(seeds[5], N_ROW * N_COL)).reshape((N_ROW, N_COL, FACE)).astype(jnp.int32),
        "south_map": jax.vmap(lambda own: jax.random.permutation(own, FACE))(jax.random.split(seeds[6], N_ROW * N_COL)).reshape((N_ROW, N_COL, FACE)).astype(jnp.int32),
        "prim_local": with_ends(jax.random.randint(seeds[7], (N_ROW, N_COL, NPRIM), 0, NI), jax.random.fold_in(seeds[7], 1), 0, NI - 1).astype(jnp.int32),
        "prim_coarse": with_ends(jax.random.randint(seeds[8], (N_ROW, N_COL, NPRIM), 0, NCO), jax.random.fold_in(seeds[8], 1), 0, NCO - 1).astype(jnp.int32),
    }


HIGHEST_PRECISION = lax.Precision.HIGHEST


def face_weights():
    face_ids = jnp.arange(NI) // FACE
    column_ids = jnp.arange(N_COL)
    row_ids = jnp.arange(N_ROW)
    neighbour_flags = jnp.stack([
        jnp.broadcast_to(column_ids[None, :] > 0, (N_ROW, N_COL)),
        jnp.broadcast_to(column_ids[None, :] < N_COL - 1, (N_ROW, N_COL)),
        jnp.broadcast_to(row_ids[:, None] > 0, (N_ROW, N_COL)),
        jnp.broadcast_to(row_ids[:, None] < N_ROW - 1, (N_ROW, N_COL))], axis=-1)
    return jnp.where(neighbour_flags[:, :, face_ids], 0.5, 1.0).astype(jnp.float32)[..., None]


def pick_rows(values, orders):
    return jax.vmap(jax.vmap(lambda source, places: jnp.take(source, places, axis=0)))(values, orders)


def place_rows(values, orders):
    return jax.vmap(jax.vmap(lambda source, places: jnp.zeros_like(source).at[places].set(source)))(values, orders)


def assemble(values, west_map, south_map):
    west_face = values[:, :, :FACE]
    east_face = values[:, :, FACE:2 * FACE]
    south_face = values[:, :, 2 * FACE:3 * FACE]
    north_face = values[:, :, 3 * FACE:]
    blank_column = jnp.zeros((N_ROW, 1, FACE, NRHS), jnp.float32)
    blank_row = jnp.zeros((1, N_COL, FACE, NRHS), jnp.float32)
    from_west = jnp.concatenate([blank_column, east_face[:, :-1]], axis=1)
    west_add = pick_rows(from_west, west_map)
    from_east = jnp.concatenate([place_rows(west_face, west_map)[:, 1:], blank_column], axis=1)
    from_south = jnp.concatenate([blank_row, north_face[:-1]], axis=0)
    south_add = pick_rows(from_south, south_map)
    from_north = jnp.concatenate([place_rows(south_face, south_map)[1:], blank_row], axis=0)
    return values + jnp.concatenate([west_add, from_east, south_add, from_north], axis=2)


def local_solve(operands):
    schur_block, factor_block, scaled, sweeps = operands
    first = jnp.dot(factor_block, scaled, precision=HIGHEST_PRECISION, preferred_element_type=jnp.float32)

    def sweep(turn, current):
        inner_term = jnp.dot(schur_block, current, precision=HIGHEST_PRECISION, preferred_element_type=jnp.float32)
        return current + jnp.dot(factor_block, scaled - inner_term, precision=HIGHEST_PRECISION, preferred_element_type=jnp.float32)

    return lax.fori_loop(1, sweeps, sweep, first)


def coarse_part(scaled, prim_local, prim_coarse, coarse_inverse):
    picked = pick_rows(scaled, prim_local)
    right_side = jnp.zeros((NCO, NRHS), jnp.float32).at[prim_coarse.reshape(-1)].add(picked.reshape(-1, NRHS))
    solved = jnp.dot(coarse_inverse, right_side, precision=HIGHEST_PRECISION, preferred_element_type=jnp.float32)
    spread = jnp.take(solved, prim_coarse.reshape(-1), axis=0).reshape(N_ROW, N_COL, NPRIM, NRHS)
    return jax.vmap(jax.vmap(lambda source, places: jnp.zeros((NI, NRHS), jnp.float32).at[places].add(source)))(spread, prim_local)


def reference(loads, schur, factor, coarse_inverse, elements, west_map, south_map, prim_local, prim_coarse):
    weights = face_weights()
    sweep_count = elements // ELEM_BASE

    def operator(values):
        return assemble(jnp.matmul(schur, values, precision=HIGHEST_PRECISION), west_map, south_map)

    def precondition(current):
        scaled = weights * current
        local = lax.map(local_solve, (schur.reshape(-1, NI, NI), factor.reshape(-1, NI, NI),
                                      scaled.reshape(-1, NI, NRHS), sweep_count.reshape(-1)))
        local = local.reshape(N_ROW, N_COL, NI, NRHS)
        correction = coarse_part(scaled, prim_local, prim_coarse, coarse_inverse)
        return assemble(weights * (local + correction), west_map, south_map)

    def inner(first, second):
        return jnp.sum(weights * first * second, axis=(0, 1, 2))

    right_side = assemble(loads, west_map, south_map)
    solution = jnp.zeros_like(right_side)
    residual = right_side
    precond = precondition(residual)
    direction = precond
    product_now = inner(residual, precond)
    for iteration in range(ITERS):
        image = operator(direction)
        alpha = product_now / inner(direction, image)
        solution = solution + alpha * direction
        residual = residual - alpha * image
        if iteration + 1 < ITERS:
            precond = precondition(residual)
            product_next = inner(residual, precond)
            direction = precond + (product_next / product_now) * direction
            product_now = product_next
    return solution, residual
```

```python
import functools

import jax
import jax.numpy as jnp
from jax import lax
from jax.experimental import pallas as pl
from jax.experimental.pallas import tpu as pltpu
from jax.sharding import PartitionSpec as P

ELEM_BASE = 4096
MOST_SWEEPS = 3
MESH = pl.DeviceIdType.MESH
F32, BF16 = jnp.float32, jnp.bfloat16
NT = (((1,), (1,)), ((), ()))
IDX, RHS, SOL, SUM = range(4)


def split(values):
    high = values.astype(BF16).astype(F32)
    return jnp.concatenate([high, values - high], axis=0).astype(BF16)


def join(stacked):
    rows = stacked.shape[0] // 2
    return stacked[:rows] + stacked[rows:]


def dot(a, b):
    return jnp.dot(a, b, preferred_element_type=F32)


def dot_nt(a, b):
    return lax.dot_general(a, b, NT, preferred_element_type=F32)


def kernel(
    n_row, n_col, loads, schur_hbm, factor_hbm, coarse_hbm, elements, west_map, south_map,
    prim_local, prim_coarse, solution, residual,
    schur_in, factor_in, coarse_in, schur_hi, schur_lo, factor_hi, factor_lo,
    coarse_split, cols_hi, cols_lo, west_hot, south_hot, local_hot, coarse_hot,
    place, idx_row, idx_col, val_row, val_col, sum_row, sum_col,
    face_out, face_in, kept,
    copy_sem, face_send, face_recv, row_send, row_recv, col_send, col_recv,
):
    a, c = lax.axis_index("row"), lax.axis_index("col")
    unknowns = loads.shape[1]
    face = unknowns // 4
    wide = local_hot.shape[1]
    coarse_rows, coarse_all = coarse_in.shape
    nprim = prim_local.shape[1]

    copies = [
        pltpu.make_async_copy(src, dst, copy_sem.at[i])
        for i, (src, dst) in enumerate(
            [(factor_hbm, factor_in), (coarse_hbm, coarse_in), (schur_hbm, schur_in)]
        )
    ]
    barrier = pltpu.get_barrier_semaphore()
    for d in range(1, n_row):
        pl.semaphore_signal(barrier, inc=1, device_id=(lax.rem(a + d, n_row), c), device_id_type=MESH)
    for d in range(1, n_col):
        pl.semaphore_signal(barrier, inc=1, device_id=(a, lax.rem(c + d, n_col)), device_id_type=MESH)
    for copy in copies:
        copy.start()

    def hot(order_ref):
        return (
            lax.broadcasted_iota(jnp.int32, (face, face), 0) == order_ref[...]
        ).astype(F32).astype(BF16)

    west_hot[...] = hot(west_map)
    south_hot[...] = hot(south_map)

    def placed(source):
        place[...] = jnp.full(place.shape, -1, jnp.int32)
        place[:1, :nprim] = source[...]
        base = place[...]
        out = base
        for i in range(1, n_row):
            out = jnp.where(a == i, pltpu.roll(base, nprim * i, 1), out)
        return out[:1]

    own_coarse = placed(prim_coarse)
    own_local = placed(prim_local)
    idx_row[a] = own_coarse

    lane = lax.broadcasted_iota(jnp.int32, (1, unknowns), 1)
    flags = [c > 0, c < n_col - 1, a > 0, a < n_row - 1]
    halves = [jnp.where(flag, 0.5, 1.0).astype(F32) for flag in flags]
    weights = jnp.where(
        lane < face,
        halves[0],
        jnp.where(lane < 2 * face, halves[1], jnp.where(lane < 3 * face, halves[2], halves[3])),
    )
    targets = [(a, c + 1), (a, c - 1), (a + 1, c), (a - 1, c)]
    can_send = [flags[1], flags[0], flags[3], flags[2]]

    def face_copy(turn, slot):
        return pltpu.make_async_remote_copy(
            src_ref=face_out.at[turn, slot],
            dst_ref=face_in.at[turn, slot],
            send_sem=face_send.at[turn, slot],
            recv_sem=face_recv.at[turn, slot],
            device_id=targets[slot],
            device_id_type=MESH,
        )

    def face_fill(turn, values):
        face_out[turn, 0] = values[:, face : 2 * face]
        face_out[turn, 2] = values[:, 3 * face :]
        face_out[turn, 1] = join(dot_nt(split(values[:, :face]), west_hot[...]))
        face_out[turn, 3] = join(dot_nt(split(values[:, 2 * face : 3 * face]), south_hot[...]))

    def face_start(turn):
        for slot in range(4):
            @pl.when(can_send[slot])
            def _():
                face_copy(turn, slot).start()

    def face_finish(turn, values):
        for slot in range(4):
            @pl.when(flags[slot])
            def _():
                face_copy(turn, slot).wait_recv()

            @pl.when(jnp.logical_not(flags[slot]))
            def _():
                face_in[turn, slot] = jnp.zeros(face_in.shape[2:], F32)
        adds = [
            join(dot(split(face_in[turn, 0]), west_hot[...])),
            face_in[turn, 1],
            join(dot(split(face_in[turn, 2]), south_hot[...])),
            face_in[turn, 3],
        ]
        return values + jnp.concatenate(adds, axis=1)

    def spread(buffer, kind, along_row):
        n = n_row if along_row else n_col
        me = a if along_row else c
        sends, recvs = (row_send, row_recv) if along_row else (col_send, col_recv)
        out = []
        for d in range(1, n):
            peer = lax.rem(me + d, n)
            out.append(
                pltpu.make_async_remote_copy(
                    src_ref=buffer.at[me],
                    dst_ref=buffer.at[me],
                    send_sem=sends.at[kind, d],
                    recv_sem=recvs.at[kind, d],
                    device_id=(peer, c) if along_row else (a, peer),
                    device_id_type=MESH,
                )
            )
        return out

    started = []

    def start(group):
        for copy in group:
            copy.start()
        started.extend(group)
        return group

    def arrive(group):
        for copy in group:
            copy.wait_recv()

    def total(buffer, n):
        out = buffer[0]
        for i in range(1, n):
            out = out + buffer[i]
        return out

    first = loads[...]
    face_fill(0, first)
    pl.semaphore_wait(barrier, n_row + n_col - 2)
    face_start(0)
    idx_rows = start(spread(idx_row, IDX, True))

    rows_iota = lax.broadcasted_iota(jnp.int32, (unknowns, wide), 0)
    local_hot[...] = (rows_iota == own_local).astype(F32).astype(BF16)

    def split_matrix(source, high, low):
        step = 128

        def one(i, carry):
            at = pl.ds(pl.multiple_of(i * step, step), step)
            values = source[at, :]
            top = values.astype(BF16)
            high[at, :] = top
            low[at, :] = (values - top.astype(F32)).astype(BF16)
            return carry

        lax.fori_loop(0, source.shape[0] // step, one, 0)

    copies[0].wait()
    split_matrix(factor_in, factor_hi, factor_lo)

    arrive(idx_rows)
    merged = idx_row[0]
    for i in range(1, n_row):
        merged = jnp.maximum(merged, idx_row[i])
    idx_col[c] = merged
    idx_cols = start(spread(idx_col, IDX, False))

    right_side = face_finish(0, first)
    scaled = weights * right_side
    val_row[0, a] = join(dot(split(scaled), local_hot[...]))
    group = start(spread(val_row.at[0], RHS, True))

    def apply(high, low, vectors):
        both = split(vectors)
        return join(dot(both, high[...]) + dot(both, low[...]))

    local = apply(factor_hi, factor_lo, scaled)

    arrive(group)
    val_col[0, c] = total(val_row.at[0], n_row)
    group = start(spread(val_col.at[0], RHS, False))

    copies[1].wait()
    coarse_split[...] = split(coarse_in[...])
    arrive(idx_cols)
    chunk = 512 if coarse_all % 512 == 0 else 128

    def one_column(s, carry):
        wanted = idx_col[s]

        def one_chunk(k, acc):
            start_at = pl.multiple_of(k * chunk, chunk)
            here = lax.broadcasted_iota(jnp.int32, (chunk, wide), 0) + start_at
            picks = (here == wanted).astype(F32).astype(BF16)
            return acc + dot(coarse_split[:, pl.ds(start_at, chunk)], picks)

        acc = lax.fori_loop(
            0, coarse_all // chunk, one_chunk, jnp.zeros((2 * coarse_rows, wide), F32)
        )
        values = join(acc)
        top = values.astype(BF16)
        cols_hi[s] = top
        cols_lo[s] = (values - top.astype(F32)).astype(BF16)
        return carry

    lax.fori_loop(0, n_col, one_column, 0)

    arrive(group)
    solved = jnp.zeros((16, coarse_rows), F32)
    for s in range(n_col):
        terms = split(val_col[0, s])
        solved = solved + dot_nt(terms, cols_hi[s]) + dot_nt(terms, cols_lo[s])
    kept[...] = jnp.zeros(kept.shape, F32)
    kept[:, :coarse_rows] = join(solved)
    base = kept[...]
    moved = base
    for i in range(1, n_row):
        moved = jnp.where(a == i, pltpu.roll(base, coarse_rows * i, 1), moved)
    val_row[1, a] = moved
    group = start(spread(val_row.at[1], SOL, True))

    copies[2].wait()
    split_matrix(schur_in, schur_hi, schur_lo)

    def one_pick(s, carry):
        at = lax.broadcasted_iota(jnp.int32, (wide, wide), 0)
        block = jnp.zeros((wide, wide), jnp.int32)
        for i in range(1, n_row):
            block = block + (at >= coarse_rows * i).astype(jnp.int32)
        number = (block * n_col + s) * coarse_rows + at - block * coarse_rows
        number = jnp.where(at < n_row * coarse_rows, number, -2)
        coarse_hot[pl.ds(pl.multiple_of(s * wide, wide), wide), :] = (
            (number == own_coarse).astype(F32).astype(BF16)
        )
        return carry

    lax.fori_loop(0, n_col, one_pick, 0)

    arrive(group)
    val_col[1, c] = total(val_row.at[1], n_row)
    group = start(spread(val_col.at[1], SOL, False))

    for turn in range(2, MOST_SWEEPS + 1):
        inner = scaled - apply(schur_hi, schur_lo, local)
        later = local + apply(factor_hi, factor_lo, inner)
        more = jnp.broadcast_to(elements[...], local.shape) >= turn * ELEM_BASE
        local = jnp.where(more, later, local)

    arrive(group)
    read = jnp.zeros((16, wide), F32)
    for s in range(n_col):
        read = read + dot(split(val_col[1, s]), coarse_hot[s * wide : (s + 1) * wide, :])
    correction = join(dot_nt(split(join(read)), local_hot[...]))
    halved = weights * (local + correction)
    face_fill(1, halved)
    face_start(1)

    def lane_sum(values):
        return jnp.sum(values, axis=1, keepdims=True)

    rz = lane_sum(right_side * halved)
    precond = face_finish(1, halved)
    image = apply(schur_hi, schur_lo, precond)
    face_fill(2, image)
    face_start(2)
    pq = lane_sum(precond * image)
    sum_lane = lax.broadcasted_iota(jnp.int32, sum_row.shape[1:], 1)
    sum_row[a] = jnp.where(sum_lane == 0, rz, pq)
    group = start(spread(sum_row, SUM, True))
    arrive(group)
    sum_col[c] = total(sum_row, n_row)
    group = start(spread(sum_col, SUM, False))
    image = face_finish(2, image)
    arrive(group)
    sums = total(sum_col, n_col)
    alpha = sums[:, :1] / sums[:, 1:2]
    solution[...] = alpha * precond
    residual[...] = right_side - alpha * image

    for copy in started:
        copy.wait_send()
    for turn in range(3):
        for slot in range(4):
            @pl.when(can_send[slot])
            def _():
                face_copy(turn, slot).wait_send()


def up(n, to):
    return -(-n // to) * to


def body(
    n_row, n_col, loads, schur, factor, coarse_inverse, elements, west_map, south_map,
    prim_local, prim_coarse,
):
    vectors = loads[0, 0].T
    rhs, unknowns = vectors.shape
    face = unknowns // 4
    coarse_rows, coarse_all = coarse_inverse.shape
    nprim = prim_local.shape[2]
    wide = up(n_row * max(nprim, coarse_rows), 128)
    vmem = pl.BlockSpec(memory_space=pltpu.VMEM)
    hbm = pl.BlockSpec(memory_space=pl.ANY)
    dma = pltpu.SemaphoreType.DMA
    out = jax.ShapeDtypeStruct(vectors.shape, F32)
    solution, residual = pl.pallas_call(
        functools.partial(kernel, n_row, n_col),
        out_shape=(out, out),
        in_specs=[vmem, hbm, hbm, hbm, vmem, vmem, vmem, vmem, vmem],
        out_specs=(vmem, vmem),
        scratch_shapes=[
            pltpu.VMEM((unknowns, unknowns), F32),
            pltpu.VMEM((unknowns, unknowns), F32),
            pltpu.VMEM((coarse_rows, coarse_all), F32),
            pltpu.VMEM((unknowns, unknowns), BF16),
            pltpu.VMEM((unknowns, unknowns), BF16),
            pltpu.VMEM((unknowns, unknowns), BF16),
            pltpu.VMEM((unknowns, unknowns), BF16),
            pltpu.VMEM((2 * coarse_rows, coarse_all), BF16),
            pltpu.VMEM((n_col, coarse_rows, wide), BF16),
            pltpu.VMEM((n_col, coarse_rows, wide), BF16),
            pltpu.VMEM((face, face), BF16),
            pltpu.VMEM((face, face), BF16),
            pltpu.VMEM((unknowns, wide), BF16),
            pltpu.VMEM((n_col * wide, wide), BF16),
            pltpu.VMEM((8, wide), jnp.int32),
            pltpu.VMEM((n_row, 1, wide), jnp.int32),
            pltpu.VMEM((n_col, 1, wide), jnp.int32),
            pltpu.VMEM((2, n_row, rhs, wide), F32),
            pltpu.VMEM((2, n_col, rhs, wide), F32),
            pltpu.VMEM((n_row, rhs, 128), F32),
            pltpu.VMEM((n_col, rhs, 128), F32),
            pltpu.VMEM((3, 4, rhs, face), F32),
            pltpu.VMEM((3, 4, rhs, face), F32),
            pltpu.VMEM((rhs, wide), F32),
            dma((3,)),
            dma((3, 4)),
            dma((3, 4)),
            dma((4, n_row)),
            dma((4, n_row)),
            dma((4, n_col)),
            dma((4, n_col)),
        ],
        compiler_params=pltpu.CompilerParams(collective_id=0, has_side_effects=True),
    )(
        vectors, schur[0, 0], factor[0, 0], coarse_inverse, elements,
        west_map[0], south_map[0], prim_local[0], prim_coarse[0],
    )
    return solution.T[None, None], residual.T[None, None]


def solution(mesh):
    placed = (
        P("row", "col", None, None),
        P("row", "col", None, None),
        P("row", "col", None, None),
        P(("row", "col"), None),
        P("row", "col"),
        P("row", "col", None),
        P("row", "col", None),
        P("row", "col", None),
        P("row", "col", None),
    )
    return jax.shard_map(
        functools.partial(body, mesh.shape["row"], mesh.shape["col"]),
        mesh=mesh,
        in_specs=placed,
        out_specs=(P("row", "col", None, None), P("row", "col", None, None)),
        check_vma=False,
    )
```

```python
import functools

import jax
import jax.numpy as jnp
from jax import lax
from jax.experimental import pallas as pl
from jax.experimental.pallas import tpu as pltpu
from jax.sharding import PartitionSpec as P

ELEM_BASE = 4096
MOST_SWEEPS = 3
MESH = pl.DeviceIdType.MESH
F32, BF16 = jnp.float32, jnp.bfloat16
NT = (((1,), (1,)), ((), ()))
IDX, RHS, SOL, SUM = range(4)


def split(values):
    high = values.astype(BF16).astype(F32)
    return jnp.concatenate([high, values - high], axis=0).astype(BF16)


def join(stacked):
    rows = stacked.shape[0] // 2
    return stacked[:rows] + stacked[rows:]


def one_hot(numbers, wanted):
    return jnp.where(numbers == wanted, 1.0, 0.0).astype(BF16)


def dot(a, b):
    return jnp.dot(a, b, preferred_element_type=F32)


def dot_nt(a, b):
    return lax.dot_general(a, b, NT, preferred_element_type=F32)


def kernel(
    n_row, n_col, loads, schur_hbm, factor_hbm, coarse_hbm, elements, west_map, south_map,
    prim_local, prim_coarse, direction, image_out, loads_out, alpha_out,
    schur_in, factor_in, coarse_in, schur_hi, schur_lo, factor_hi, factor_lo,
    coarse_split, columns, west_hot, south_hot, local_hot, coarse_hot,
    place, idx_all, val_all, sum_all, face_out, face_in,
    copy_sem, face_send, face_recv, all_send, all_recv,
):
    a, c = lax.axis_index("row"), lax.axis_index("col")
    unknowns = loads.shape[1]
    face = unknowns // 4
    wide = local_hot.shape[1]
    half = wide // 2
    count = n_row * n_col
    me = a * n_col + c
    odd = lax.rem(me, 2)
    coarse_rows, coarse_all = coarse_in.shape
    nprim = prim_local.shape[1]

    copies = [
        pltpu.make_async_copy(src, dst, copy_sem.at[i])
        for i, (src, dst) in enumerate(
            [(factor_hbm, factor_in), (coarse_hbm, coarse_in), (schur_hbm, schur_in)]
        )
    ]
    barrier = pltpu.get_barrier_semaphore()
    def peer(d):
        other = lax.rem(me + d, count)
        return (lax.div(other, n_col), lax.rem(other, n_col))

    def each(work):
        if count <= 64:
            for d in range(1, count):
                work(d)
        else:
            lax.fori_loop(1, count, lambda d, carry: (work(d), carry)[1], 0)

    each(lambda d: pl.semaphore_signal(barrier, inc=1, device_id=peer(d), device_id_type=MESH))
    for copy in copies:
        copy.start()

    def hot(order_ref):
        return one_hot(lax.broadcasted_iota(jnp.int32, (face, face), 0), order_ref[...])

    west_hot[...] = hot(west_map)
    south_hot[...] = hot(south_map)

    def placed(source):
        place[...] = jnp.full(place.shape, -1, jnp.int32)
        place[:1, :nprim] = source[...]
        base = place[...]
        return jnp.where(odd == 1, pltpu.roll(base, half, 1), base)[:1]

    own_coarse = placed(prim_coarse)
    own_local = placed(prim_local)
    idx_all[me] = own_coarse

    lane = lax.broadcasted_iota(jnp.int32, (1, unknowns), 1)
    flags = [c > 0, c < n_col - 1, a > 0, a < n_row - 1]
    halves = [jnp.where(flag, 0.5, 1.0).astype(F32) for flag in flags]
    weights = jnp.where(
        lane < face,
        halves[0],
        jnp.where(lane < 2 * face, halves[1], jnp.where(lane < 3 * face, halves[2], halves[3])),
    )
    targets = [(a, c + 1), (a, c - 1), (a + 1, c), (a - 1, c)]
    can_send = [flags[1], flags[0], flags[3], flags[2]]

    def face_copy(turn, slot):
        return pltpu.make_async_remote_copy(
            src_ref=face_out.at[turn, slot],
            dst_ref=face_in.at[turn, slot],
            send_sem=face_send.at[turn, slot],
            recv_sem=face_recv.at[turn, slot],
            device_id=targets[slot],
            device_id_type=MESH,
        )

    def face_fill(turn, values):
        face_out[turn, 0] = values[:, face : 2 * face]
        face_out[turn, 2] = values[:, 3 * face :]
        face_out[turn, 1] = join(dot_nt(split(values[:, :face]), west_hot[...]))
        face_out[turn, 3] = join(dot_nt(split(values[:, 2 * face : 3 * face]), south_hot[...]))

    def face_start(turn):
        for slot in range(4):
            @pl.when(can_send[slot])
            def _():
                face_copy(turn, slot).start()

    def face_finish(turn, values):
        for slot in range(4):
            @pl.when(flags[slot])
            def _():
                face_copy(turn, slot).wait_recv()

            @pl.when(jnp.logical_not(flags[slot]))
            def _():
                face_in[turn, slot] = jnp.zeros(face_in.shape[2:], F32)
        adds = [
            join(dot(split(face_in[turn, 0]), west_hot[...])),
            face_in[turn, 1],
            join(dot(split(face_in[turn, 2]), south_hot[...])),
            face_in[turn, 3],
        ]
        return values + jnp.concatenate(adds, axis=1)

    def all_copy(buffer, kind, d):
        return pltpu.make_async_remote_copy(
            src_ref=buffer.at[me],
            dst_ref=buffer.at[me],
            send_sem=all_send.at[kind, d],
            recv_sem=all_recv.at[kind, d],
            device_id=peer(d),
            device_id_type=MESH,
        )

    def start(buffer, kind):
        each(lambda d: all_copy(buffer, kind, d).start())

    def arrive(buffer, kind):
        each(lambda d: all_copy(buffer, kind, d).wait_recv())

    def pairs(buffer, s, merge):
        return jnp.concatenate(
            [merge(buffer[4 * s + 2 * i], buffer[4 * s + 2 * i + 1]) for i in range(2)], axis=1
        )

    first = loads[...]
    face_fill(0, first)
    pl.semaphore_wait(barrier, count - 1)
    face_start(0)
    start(idx_all, IDX)

    rows_iota = lax.broadcasted_iota(jnp.int32, (unknowns, wide), 0)
    local_hot[...] = one_hot(rows_iota, own_local)

    def split_matrix(source, high, low):
        step = 128

        def one(i, carry):
            at = pl.ds(pl.multiple_of(i * step, step), step)
            values = source[at, :]
            top = values.astype(BF16)
            high[at, :] = top
            low[at, :] = (values - top.astype(F32)).astype(BF16)
            return carry

        lax.fori_loop(0, source.shape[0] // step, one, 0)

    copies[0].wait()
    split_matrix(factor_in, factor_hi, factor_lo)

    right_side = face_finish(0, first)
    scaled = weights * right_side
    val_all[0, me] = join(dot(split(scaled), local_hot[...]))
    start(val_all.at[0], RHS)

    def apply(high, low, vectors):
        both = split(vectors)
        return join(dot(both, high[...]) + dot(both, low[...]))

    local = apply(factor_hi, factor_lo, scaled)

    copies[1].wait()
    values = coarse_in[...]
    top = values.astype(BF16)
    coarse_split[...] = jnp.zeros(coarse_split.shape, BF16)
    coarse_split[:coarse_rows, :] = top
    coarse_split[half : half + coarse_rows, :] = (values - top.astype(F32)).astype(BF16)
    arrive(idx_all, IDX)
    chunk = 256
    chunks = coarse_all // chunk
    small = lax.broadcasted_iota(jnp.int32, (chunk, 2 * wide), 0).astype(F32).astype(BF16)

    def one_column(s, carry):
        wanted = pairs(idx_all, s, jnp.maximum)

        def one_chunk(k, acc):
            start_at = k * chunk
            offset = wanted - start_at
            inside = jnp.logical_and(offset >= 0, offset < chunk)
            offset = jnp.where(inside, offset, -1).astype(F32).astype(BF16)
            picks = jnp.where(small == offset, jnp.ones_like(small), jnp.zeros_like(small))
            return acc + dot(coarse_split[:, pl.ds(start_at, chunk)], picks)

        acc = jnp.zeros((wide, 2 * wide), F32)
        if chunks <= 8:
            for k in range(chunks):
                acc = one_chunk(k, acc)
        else:
            acc = lax.fori_loop(
                0, chunks, lambda k, acc: one_chunk(pl.multiple_of(k, 1), acc), acc
            )
        values = join(acc)
        top = values.astype(BF16)
        at = pl.ds(pl.multiple_of(s * 2 * wide, 2 * wide), 2 * wide)
        columns[:half, at] = top
        columns[half:, at] = (values - top.astype(F32)).astype(BF16)
        return carry

    lax.fori_loop(0, count // 4, one_column, 0)

    def gathered(buffer):
        return split(
            jnp.concatenate([pairs(buffer, s, jnp.add) for s in range(count // 4)], axis=1)
        )

    arrive(val_all.at[0], RHS)
    solved = join(dot_nt(gathered(val_all.at[0]), columns[...]))
    solved = solved + pltpu.roll(solved, half, 1)
    wide_lane = lax.broadcasted_iota(jnp.int32, solved.shape, 1)
    lowest = odd * half
    mine = jnp.logical_and(wide_lane >= lowest, wide_lane < lowest + half)
    val_all[1, me] = jnp.where(mine, solved, 0.0)
    start(val_all.at[1], SOL)

    copies[2].wait()
    split_matrix(schur_in, schur_hi, schur_lo)

    at = lax.broadcasted_iota(jnp.int32, (wide, wide), 0)
    upper = (at >= half).astype(jnp.int32)
    number = upper * coarse_rows + at - upper * half
    number = jnp.where(at - upper * half < coarse_rows, number, -2 * coarse_all)

    def one_pick(s, carry):
        coarse_hot[pl.ds(pl.multiple_of(s * wide, wide), wide), :] = one_hot(
            number, own_coarse - s * 2 * coarse_rows
        )
        return carry

    lax.fori_loop(0, count // 2, one_pick, 0)

    for turn in range(2, MOST_SWEEPS + 1):
        inner = scaled - apply(schur_hi, schur_lo, local)
        later = local + apply(factor_hi, factor_lo, inner)
        more = jnp.broadcast_to(elements[...], local.shape) >= turn * ELEM_BASE
        local = jnp.where(more, later, local)

    arrive(val_all.at[1], SOL)
    read = join(dot(gathered(val_all.at[1]), coarse_hot[...]))
    correction = join(dot_nt(split(read), local_hot[...]))
    halved = weights * (local + correction)
    face_fill(1, halved)
    face_start(1)

    def lane_sum(values):
        return jnp.sum(values, axis=1, keepdims=True)

    rz = lane_sum(right_side * halved)
    precond = face_finish(1, halved)
    image = apply(schur_hi, schur_lo, precond)
    face_fill(2, image)
    face_start(2)
    pq = lane_sum(precond * image)
    sum_lane = lax.broadcasted_iota(jnp.int32, sum_all.shape[1:], 1)
    sum_all[me] = jnp.where(sum_lane == 0, rz, pq)
    start(sum_all, SUM)
    direction[...] = precond
    loads_out[...] = right_side
    image_out[...] = face_finish(2, image)
    arrive(sum_all, SUM)
    sums = sum_all[0]
    for i in range(1, count):
        sums = sums + sum_all[i]
    alpha_out[...] = jnp.broadcast_to(sums[:, :1] / sums[:, 1:2], alpha_out.shape)

    for kind, buffer in enumerate([idx_all, val_all.at[0], val_all.at[1], sum_all]):
        each(lambda d: all_copy(buffer, kind, d).wait_send())
    for turn in range(3):
        for slot in range(4):
            @pl.when(can_send[slot])
            def _():
                face_copy(turn, slot).wait_send()


def up(n, to):
    return -(-n // to) * to


def body(
    n_row, n_col, loads, schur, factor, coarse_inverse, elements, west_map, south_map,
    prim_local, prim_coarse,
):
    vectors = loads[0, 0].T
    rhs, unknowns = vectors.shape
    face = unknowns // 4
    coarse_rows, coarse_all = coarse_inverse.shape
    nprim = prim_local.shape[2]
    wide = 2 * up(max(nprim, coarse_rows), 64)
    count = n_row * n_col
    vmem = pl.BlockSpec(memory_space=pltpu.VMEM)
    hbm = pl.BlockSpec(memory_space=pl.ANY)
    dma = pltpu.SemaphoreType.DMA
    out = jax.ShapeDtypeStruct(vectors.shape, F32)
    direction, image, right_side, alpha = pl.pallas_call(
        functools.partial(kernel, n_row, n_col),
        out_shape=(out, out, out, out),
        in_specs=[vmem, hbm, hbm, hbm, vmem, vmem, vmem, vmem, vmem],
        out_specs=(vmem, vmem, vmem, vmem),
        scratch_shapes=[
            pltpu.VMEM((unknowns, unknowns), F32),
            pltpu.VMEM((unknowns, unknowns), F32),
            pltpu.VMEM((coarse_rows, coarse_all), F32),
            pltpu.VMEM((unknowns, unknowns), BF16),
            pltpu.VMEM((unknowns, unknowns), BF16),
            pltpu.VMEM((unknowns, unknowns), BF16),
            pltpu.VMEM((unknowns, unknowns), BF16),
            pltpu.VMEM((wide, coarse_all), BF16),
            pltpu.VMEM((wide, count // 2 * wide), BF16),
            pltpu.VMEM((face, face), BF16),
            pltpu.VMEM((face, face), BF16),
            pltpu.VMEM((unknowns, wide), BF16),
            pltpu.VMEM((count // 2 * wide, wide), BF16),
            pltpu.VMEM((8, wide), jnp.int32),
            pltpu.VMEM((count, 1, wide), jnp.int32),
            pltpu.VMEM((2, count, rhs, wide), F32),
            pltpu.VMEM((count, rhs, 128), F32),
            pltpu.VMEM((3, 4, rhs, face), F32),
            pltpu.VMEM((3, 4, rhs, face), F32),
            dma((3,)),
            dma((3, 4)),
            dma((3, 4)),
            dma((4, count)),
            dma((4, count)),
        ],
        compiler_params=pltpu.CompilerParams(collective_id=0, has_side_effects=True),
    )(
        vectors, schur[0, 0], factor[0, 0], coarse_inverse, elements,
        west_map[0], south_map[0], prim_local[0], prim_coarse[0],
    )
    solution = alpha * direction
    residual = right_side - alpha * image
    return solution.T[None, None], residual.T[None, None]


def solution(mesh):
    placed = (
        P("row", "col", None, None),
        P("row", "col", None, None),
        P("row", "col", None, None),
        P(("row", "col"), None),
        P("row", "col"),
        P("row", "col", None),
        P("row", "col", None),
        P("row", "col", None),
        P("row", "col", None),
    )
    return jax.shard_map(
        functools.partial(body, mesh.shape["row"], mesh.shape["col"]),
        mesh=mesh,
        in_specs=placed,
        out_specs=(P("row", "col", None, None), P("row", "col", None, None)),
        check_vma=False,
    )
```

```python
import functools

import jax
import jax.numpy as jnp
from jax import lax
from jax.experimental import pallas as pl
from jax.experimental.pallas import tpu as pltpu
from jax.sharding import PartitionSpec as P

ELEM_BASE = 4096
MOST_SWEEPS = 3
MESH = pl.DeviceIdType.MESH
F32, BF16 = jnp.float32, jnp.bfloat16
NT = (((1,), (1,)), ((), ()))
IDX, RHS, SOL, SUM = range(4)


def split(values):
    high = values.astype(BF16).astype(F32)
    return jnp.concatenate([high, values - high], axis=0).astype(BF16)


def join(stacked):
    rows = stacked.shape[0] // 2
    return stacked[:rows] + stacked[rows:]


def one_hot(numbers, wanted):
    return jnp.where(numbers == wanted, 1.0, 0.0).astype(BF16)


def dot(a, b):
    return jnp.dot(a, b, preferred_element_type=F32)


def dot_nt(a, b):
    return lax.dot_general(a, b, NT, preferred_element_type=F32)


def kernel(
    n_row, n_col, loads, schur_hbm, factor_hbm, coarse_hbm, elements, west_map, south_map,
    prim_local, prim_coarse, direction, image_out, loads_out, alpha_out,
    schur_in, factor_in, coarse_in, schur_hi, schur_lo, factor_hi, factor_lo,
    coarse_split, columns, west_hot, south_hot, local_hot, coarse_hot,
    place, idx_all, val_all, sum_all, face_out, face_in,
    copy_sem, face_send, face_recv, all_send, all_recv,
):
    a, c = lax.axis_index("row"), lax.axis_index("col")
    unknowns = loads.shape[1]
    face = unknowns // 4
    wide = local_hot.shape[1]
    half = wide // 2
    count = n_row * n_col
    me = a * n_col + c
    odd = lax.rem(me, 2)
    coarse_rows, coarse_all = coarse_in.shape
    nprim = prim_local.shape[1]

    copies = [
        pltpu.make_async_copy(src, dst, copy_sem.at[i])
        for i, (src, dst) in enumerate(
            [(factor_hbm, factor_in), (coarse_hbm, coarse_in), (schur_hbm, schur_in)]
        )
    ]
    barrier = pltpu.get_barrier_semaphore()
    def peer(d):
        other = lax.rem(me + d, count)
        return (lax.div(other, n_col), lax.rem(other, n_col))

    def each(work):
        if count <= 64:
            for d in range(1, count):
                work(d)
        else:
            lax.fori_loop(1, count, lambda d, carry: (work(d), carry)[1], 0)

    each(lambda d: pl.semaphore_signal(barrier, inc=1, device_id=peer(d), device_id_type=MESH))
    for copy in copies:
        copy.start()

    def hot(order_ref):
        return one_hot(lax.broadcasted_iota(jnp.int32, (face, face), 0), order_ref[...])

    west_hot[...] = hot(west_map)
    south_hot[...] = hot(south_map)

    def placed(source):
        place[...] = jnp.full(place.shape, -1, jnp.int32)
        place[:1, :nprim] = source[...]
        base = place[...]
        return base, pltpu.roll(base, half, 1)

    base, rolled = placed(prim_coarse)
    own_coarse = jnp.where(odd == 1, rolled, base)[:1]
    own_local = jnp.maximum(*placed(prim_local))[:1]
    idx_all[me] = own_coarse

    lane = lax.broadcasted_iota(jnp.int32, (1, unknowns), 1)
    flags = [c > 0, c < n_col - 1, a > 0, a < n_row - 1]
    halves = [jnp.where(flag, 0.5, 1.0).astype(F32) for flag in flags]
    weights = jnp.where(
        lane < face,
        halves[0],
        jnp.where(lane < 2 * face, halves[1], jnp.where(lane < 3 * face, halves[2], halves[3])),
    )
    targets = [(a, c + 1), (a, c - 1), (a + 1, c), (a - 1, c)]
    can_send = [flags[1], flags[0], flags[3], flags[2]]

    def face_copy(turn, slot):
        return pltpu.make_async_remote_copy(
            src_ref=face_out.at[turn, slot],
            dst_ref=face_in.at[turn, slot],
            send_sem=face_send.at[turn, slot],
            recv_sem=face_recv.at[turn, slot],
            device_id=targets[slot],
            device_id_type=MESH,
        )

    def face_fill(turn, values):
        face_out[turn, 0] = values[:, face : 2 * face]
        face_out[turn, 2] = values[:, 3 * face :]
        face_out[turn, 1] = join(dot_nt(split(values[:, :face]), west_hot[...]))
        face_out[turn, 3] = join(dot_nt(split(values[:, 2 * face : 3 * face]), south_hot[...]))

    def face_start(turn):
        for slot in range(4):
            @pl.when(can_send[slot])
            def _():
                face_copy(turn, slot).start()

    def face_finish(turn, values):
        for slot in range(4):
            @pl.when(flags[slot])
            def _():
                face_copy(turn, slot).wait_recv()

            @pl.when(jnp.logical_not(flags[slot]))
            def _():
                face_in[turn, slot] = jnp.zeros(face_in.shape[2:], F32)
        adds = [
            join(dot(split(face_in[turn, 0]), west_hot[...])),
            face_in[turn, 1],
            join(dot(split(face_in[turn, 2]), south_hot[...])),
            face_in[turn, 3],
        ]
        return values + jnp.concatenate(adds, axis=1)

    def all_copy(buffer, kind, d):
        return pltpu.make_async_remote_copy(
            src_ref=buffer.at[me],
            dst_ref=buffer.at[me],
            send_sem=all_send.at[kind, d],
            recv_sem=all_recv.at[kind, d],
            device_id=peer(d),
            device_id_type=MESH,
        )

    def start(buffer, kind):
        each(lambda d: all_copy(buffer, kind, d).start())

    def arrive(buffer, kind):
        each(lambda d: all_copy(buffer, kind, d).wait_recv())

    rhs = loads.shape[0]
    lower = lax.broadcasted_iota(jnp.int32, (rhs // 2, wide), 1) < half

    def pack(values):
        return jnp.where(lower, values[: rhs // 2], values[rhs // 2 :])

    def unpack(first, second):
        both = jnp.concatenate([first, second], axis=0)
        swapped = pltpu.roll(both, half, 1)
        top = jnp.where(lower, both[: rhs // 2], swapped[rhs // 2 :])
        bottom = jnp.where(lower, swapped[: rhs // 2], both[rhs // 2 :])
        return jnp.concatenate([top, bottom], axis=0)

    first = loads[...]
    face_fill(0, first)
    pl.semaphore_wait(barrier, count - 1)
    face_start(0)
    start(idx_all, IDX)

    rows_iota = lax.broadcasted_iota(jnp.int32, (unknowns, wide), 0)
    local_hot[...] = one_hot(rows_iota, own_local)

    def split_matrix(source, high, low):
        step = 128

        def one(i, carry):
            at = pl.ds(pl.multiple_of(i * step, step), step)
            values = source[at, :]
            top = values.astype(BF16)
            high[at, :] = top
            low[at, :] = (values - top.astype(F32)).astype(BF16)
            return carry

        lax.fori_loop(0, source.shape[0] // step, one, 0)

    copies[0].wait()
    split_matrix(factor_in, factor_hi, factor_lo)

    right_side = face_finish(0, first)
    scaled = weights * right_side
    val_all[0, me] = pack(join(dot(split(scaled), local_hot[...])))
    start(val_all.at[0], RHS)

    def apply(high, low, vectors):
        both = split(vectors)
        return join(dot(both, high[...]) + dot(both, low[...]))

    local = apply(factor_hi, factor_lo, scaled)

    copies[1].wait()
    values = coarse_in[...]
    top = values.astype(BF16)
    coarse_split[...] = jnp.zeros(coarse_split.shape, BF16)
    coarse_split[:coarse_rows, :] = top
    coarse_split[half : half + coarse_rows, :] = (values - top.astype(F32)).astype(BF16)
    arrive(idx_all, IDX)
    chunk = 256
    chunks = coarse_all // chunk
    small = lax.broadcasted_iota(jnp.int32, (chunk, 2 * wide), 0).astype(F32).astype(BF16)

    def one_column(s, carry):
        wanted = jnp.concatenate(
            [jnp.maximum(idx_all[4 * s + i], idx_all[4 * s + i + 1]) for i in (0, 2)], axis=1
        )

        def one_chunk(k, acc):
            start_at = k * chunk
            offset = wanted - start_at
            inside = jnp.logical_and(offset >= 0, offset < chunk)
            offset = jnp.where(inside, offset, -1).astype(F32).astype(BF16)
            picks = jnp.where(small == offset, jnp.ones_like(small), jnp.zeros_like(small))
            return acc + dot(coarse_split[:, pl.ds(start_at, chunk)], picks)

        acc = jnp.zeros((wide, 2 * wide), F32)
        if chunks <= 8:
            for k in range(chunks):
                acc = one_chunk(k, acc)
        else:
            acc = lax.fori_loop(
                0, chunks, lambda k, acc: one_chunk(pl.multiple_of(k, 1), acc), acc
            )
        values = join(acc)
        top = values.astype(BF16)
        at = pl.ds(pl.multiple_of(s * 2 * wide, 2 * wide), 2 * wide)
        columns[:half, at] = top
        columns[half:, at] = (values - top.astype(F32)).astype(BF16)
        return carry

    lax.fori_loop(0, count // 4, one_column, 0)

    def gathered(buffer):
        return split(
            jnp.concatenate([unpack(buffer[s], buffer[s + 1]) for s in range(0, count, 2)], axis=1)
        )

    arrive(val_all.at[0], RHS)
    solved = join(dot_nt(gathered(val_all.at[0]), columns[...]))
    solved = solved + pltpu.roll(solved, half, 1)
    val_all[1, me] = pack(solved)
    start(val_all.at[1], SOL)

    copies[2].wait()
    split_matrix(schur_in, schur_hi, schur_lo)

    at = lax.broadcasted_iota(jnp.int32, (wide, wide), 0)
    upper = (at >= half).astype(jnp.int32)
    number = upper * coarse_rows + at - upper * half
    number = jnp.where(at - upper * half < coarse_rows, number, -2 * coarse_all)

    def one_pick(s, carry):
        coarse_hot[pl.ds(pl.multiple_of(s * wide, wide), wide), :] = one_hot(
            number, own_coarse - s * 2 * coarse_rows
        )
        return carry

    lax.fori_loop(0, count // 2, one_pick, 0)

    for turn in range(2, MOST_SWEEPS + 1):
        inner = scaled - apply(schur_hi, schur_lo, local)
        later = local + apply(factor_hi, factor_lo, inner)
        more = jnp.broadcast_to(elements[...], local.shape) >= turn * ELEM_BASE
        local = jnp.where(more, later, local)

    arrive(val_all.at[1], SOL)
    read = join(dot(gathered(val_all.at[1]), coarse_hot[...]))
    correction = join(dot_nt(split(read), local_hot[...]))
    halved = weights * (local + correction)
    face_fill(1, halved)
    face_start(1)

    def lane_sum(values):
        return jnp.sum(values, axis=1, keepdims=True)

    rz = lane_sum(right_side * halved)
    precond = face_finish(1, halved)
    image = apply(schur_hi, schur_lo, precond)
    face_fill(2, image)
    face_start(2)
    pq = lane_sum(precond * image)
    sum_lane = lax.broadcasted_iota(jnp.int32, (rhs, 128), 1)
    sum_case = lax.broadcasted_iota(jnp.int32, (rhs, 128), 0)
    upper_lane, lower_lane = sum_lane == sum_case + rhs, sum_lane == sum_case
    laid = jnp.where(lower_lane, rz, 0.0) + jnp.where(upper_lane, pq, 0.0)
    sum_all[me] = jnp.sum(laid, axis=0, keepdims=True)
    start(sum_all, SUM)
    direction[...] = precond
    loads_out[...] = right_side
    image_out[...] = face_finish(2, image)
    arrive(sum_all, SUM)
    sums = sum_all[0]
    for i in range(1, count):
        sums = sums + sum_all[i]
    sums = jnp.broadcast_to(sums, (rhs, 128))
    alpha = lane_sum(jnp.where(lower_lane, sums, 0.0)) / lane_sum(jnp.where(upper_lane, sums, 0.0))
    alpha_out[...] = jnp.broadcast_to(alpha, alpha_out.shape)

    for kind, buffer in enumerate([idx_all, val_all.at[0], val_all.at[1], sum_all]):
        each(lambda d: all_copy(buffer, kind, d).wait_send())
    for turn in range(3):
        for slot in range(4):
            @pl.when(can_send[slot])
            def _():
                face_copy(turn, slot).wait_send()


def up(n, to):
    return -(-n // to) * to


def body(
    n_row, n_col, loads, schur, factor, coarse_inverse, elements, west_map, south_map,
    prim_local, prim_coarse,
):
    vectors = loads[0, 0].T
    rhs, unknowns = vectors.shape
    face = unknowns // 4
    coarse_rows, coarse_all = coarse_inverse.shape
    nprim = prim_local.shape[2]
    wide = 2 * up(max(nprim, coarse_rows), 64)
    count = n_row * n_col
    vmem = pl.BlockSpec(memory_space=pltpu.VMEM)
    hbm = pl.BlockSpec(memory_space=pl.ANY)
    dma = pltpu.SemaphoreType.DMA
    out = jax.ShapeDtypeStruct(vectors.shape, F32)
    direction, image, right_side, alpha = pl.pallas_call(
        functools.partial(kernel, n_row, n_col),
        out_shape=(out, out, out, out),
        in_specs=[vmem, hbm, hbm, hbm, vmem, vmem, vmem, vmem, vmem],
        out_specs=(vmem, vmem, vmem, vmem),
        scratch_shapes=[
            pltpu.VMEM((unknowns, unknowns), F32),
            pltpu.VMEM((unknowns, unknowns), F32),
            pltpu.VMEM((coarse_rows, coarse_all), F32),
            pltpu.VMEM((unknowns, unknowns), BF16),
            pltpu.VMEM((unknowns, unknowns), BF16),
            pltpu.VMEM((unknowns, unknowns), BF16),
            pltpu.VMEM((unknowns, unknowns), BF16),
            pltpu.VMEM((wide, coarse_all), BF16),
            pltpu.VMEM((wide, count // 2 * wide), BF16),
            pltpu.VMEM((face, face), BF16),
            pltpu.VMEM((face, face), BF16),
            pltpu.VMEM((unknowns, wide), BF16),
            pltpu.VMEM((count // 2 * wide, wide), BF16),
            pltpu.VMEM((8, wide), jnp.int32),
            pltpu.VMEM((count, 1, wide), jnp.int32),
            pltpu.VMEM((2, count, rhs // 2, wide), F32),
            pltpu.VMEM((count, 1, 128), F32),
            pltpu.VMEM((3, 4, rhs, face), F32),
            pltpu.VMEM((3, 4, rhs, face), F32),
            dma((3,)),
            dma((3, 4)),
            dma((3, 4)),
            dma((4, count)),
            dma((4, count)),
        ],
        compiler_params=pltpu.CompilerParams(collective_id=0, has_side_effects=True),
    )(
        vectors, schur[0, 0], factor[0, 0], coarse_inverse, elements,
        west_map[0], south_map[0], prim_local[0], prim_coarse[0],
    )
    solution = alpha * direction
    residual = right_side - alpha * image
    return solution.T[None, None], residual.T[None, None]


def solution(mesh):
    placed = (
        P("row", "col", None, None),
        P("row", "col", None, None),
        P("row", "col", None, None),
        P(("row", "col"), None),
        P("row", "col"),
        P("row", "col", None),
        P("row", "col", None),
        P("row", "col", None),
        P("row", "col", None),
    )
    return jax.shard_map(
        functools.partial(body, mesh.shape["row"], mesh.shape["col"]),
        mesh=mesh,
        in_specs=placed,
        out_specs=(P("row", "col", None, None), P("row", "col", None, None)),
        check_vma=False,
    )
```

```python
import functools

import jax
import jax.numpy as jnp
from jax import lax
from jax.experimental import pallas as pl
from jax.experimental.pallas import tpu as pltpu
from jax.sharding import PartitionSpec as P

ELEM_BASE = 4096
MOST_SWEEPS = 3
MESH = pl.DeviceIdType.MESH
F32, BF16 = jnp.float32, jnp.bfloat16
NT = (((1,), (1,)), ((), ()))
IDX, RHS, SOL, SUM = range(4)


def split(values):
    high = values.astype(BF16).astype(F32)
    return jnp.concatenate([high, values - high], axis=0).astype(BF16)


def join(stacked):
    rows = stacked.shape[0] // 2
    return stacked[:rows] + stacked[rows:]


def one_hot(numbers, wanted):
    return jnp.where(numbers == wanted, 1.0, 0.0).astype(BF16)


def dot(a, b):
    return jnp.dot(a, b, preferred_element_type=F32)


def dot_nt(a, b):
    return lax.dot_general(a, b, NT, preferred_element_type=F32)


def kernel(
    n_row, n_col, loads, schur_hbm, factor_hbm, coarse_hbm, elements, west_map, south_map,
    prim_local, prim_coarse, direction, image_out, loads_out, alpha_out,
    schur_in, factor_in, coarse_in, schur_hi, schur_lo, factor_hi, factor_lo,
    coarse_split, columns, west_hot, south_hot, local_hot, coarse_hot,
    place, idx_all, val_all, sum_all, face_out, face_in,
    copy_sem, face_send, face_recv, all_send, all_recv,
):
    a, c = lax.axis_index("row"), lax.axis_index("col")
    unknowns = loads.shape[1]
    face = unknowns // 4
    wide = local_hot.shape[1]
    half = wide // 2
    count = n_row * n_col
    me = a * n_col + c
    odd = lax.rem(me, 2)
    coarse_rows, coarse_all = coarse_in.shape
    nprim = prim_local.shape[1]

    copies = [
        pltpu.make_async_copy(src, dst, copy_sem.at[i])
        for i, (src, dst) in enumerate(
            [(factor_hbm, factor_in), (coarse_hbm, coarse_in), (schur_hbm, schur_in)]
        )
    ]
    barrier = pltpu.get_barrier_semaphore()
    def peer(d):
        other = lax.rem(me + d, count)
        return (lax.div(other, n_col), lax.rem(other, n_col))

    def each(work):
        if count <= 64:
            for d in range(1, count):
                work(d)
        else:
            lax.fori_loop(1, count, lambda d, carry: (work(d), carry)[1], 0)

    each(lambda d: pl.semaphore_signal(barrier, inc=1, device_id=peer(d), device_id_type=MESH))
    for copy in copies:
        copy.start()

    def hot(order_ref):
        return one_hot(lax.broadcasted_iota(jnp.int32, (face, face), 0), order_ref[...])

    west_hot[...] = hot(west_map)
    south_hot[...] = hot(south_map)

    def placed(source):
        place[...] = jnp.full(place.shape, -1, jnp.int32)
        place[:1, :nprim] = source[...]
        base = place[...]
        return base, pltpu.roll(base, half, 1)

    base, rolled = placed(prim_coarse)
    own_coarse = jnp.where(odd == 1, rolled, base)[:1]
    own_local = jnp.maximum(*placed(prim_local))[:1]
    idx_all[me] = own_coarse

    lane = lax.broadcasted_iota(jnp.int32, (1, unknowns), 1)
    flags = [c > 0, c < n_col - 1, a > 0, a < n_row - 1]
    halves = [jnp.where(flag, 0.5, 1.0).astype(F32) for flag in flags]
    weights = jnp.where(
        lane < face,
        halves[0],
        jnp.where(lane < 2 * face, halves[1], jnp.where(lane < 3 * face, halves[2], halves[3])),
    )
    targets = [(a, c + 1), (a, c - 1), (a + 1, c), (a - 1, c)]
    can_send = [flags[1], flags[0], flags[3], flags[2]]

    def face_copy(turn, slot):
        return pltpu.make_async_remote_copy(
            src_ref=face_out.at[turn, slot],
            dst_ref=face_in.at[turn, slot],
            send_sem=face_send.at[turn, slot],
            recv_sem=face_recv.at[turn, slot],
            device_id=targets[slot],
            device_id_type=MESH,
        )

    def face_fill(turn, values):
        face_out[turn, 0] = values[:, face : 2 * face]
        face_out[turn, 2] = values[:, 3 * face :]
        face_out[turn, 1] = join(dot_nt(split(values[:, :face]), west_hot[...]))
        face_out[turn, 3] = join(dot_nt(split(values[:, 2 * face : 3 * face]), south_hot[...]))

    def face_start(turn):
        for slot in range(4):
            @pl.when(can_send[slot])
            def _():
                face_copy(turn, slot).start()

    def face_finish(turn, values):
        for slot in range(4):
            @pl.when(flags[slot])
            def _():
                face_copy(turn, slot).wait_recv()

            @pl.when(jnp.logical_not(flags[slot]))
            def _():
                face_in[turn, slot] = jnp.zeros(face_in.shape[2:], F32)
        adds = [
            join(dot(split(face_in[turn, 0]), west_hot[...])),
            face_in[turn, 1],
            join(dot(split(face_in[turn, 2]), south_hot[...])),
            face_in[turn, 3],
        ]
        return values + jnp.concatenate(adds, axis=1)

    def all_copy(buffer, kind, d):
        return pltpu.make_async_remote_copy(
            src_ref=buffer.at[me],
            dst_ref=buffer.at[me],
            send_sem=all_send.at[kind, d],
            recv_sem=all_recv.at[kind, d],
            device_id=peer(d),
            device_id_type=MESH,
        )

    def start(buffer, kind):
        each(lambda d: all_copy(buffer, kind, d).start())

    def arrive(buffer, kind):
        each(lambda d: all_copy(buffer, kind, d).wait_recv())

    rhs = loads.shape[0]
    lower = lax.broadcasted_iota(jnp.int32, (rhs // 2, wide), 1) < half

    def pack(values):
        return jnp.where(lower, values[: rhs // 2], values[rhs // 2 :])

    def unpack(first, second):
        both = jnp.concatenate([first, second], axis=0)
        swapped = pltpu.roll(both, half, 1)
        top = jnp.where(lower, both[: rhs // 2], swapped[rhs // 2 :])
        bottom = jnp.where(lower, swapped[: rhs // 2], both[rhs // 2 :])
        return jnp.concatenate([top, bottom], axis=0)

    first = loads[...]
    face_fill(0, first)
    pl.semaphore_wait(barrier, count - 1)
    face_start(0)
    start(idx_all, IDX)

    rows_iota = lax.broadcasted_iota(jnp.int32, (unknowns, wide), 0)
    local_hot[...] = one_hot(rows_iota, own_local)

    def split_matrix(source, high, low):
        step = 128

        def one(i, carry):
            at = pl.ds(pl.multiple_of(i * step, step), step)
            values = source[at, :]
            top = values.astype(BF16)
            high[at, :] = top
            low[at, :] = (values - top.astype(F32)).astype(BF16)
            return carry

        lax.fori_loop(0, source.shape[0] // step, one, 0)

    copies[0].wait()
    split_matrix(factor_in, factor_hi, factor_lo)

    right_side = face_finish(0, first)
    scaled = weights * right_side
    val_all[0, me] = pack(join(dot(split(scaled), local_hot[...])))
    start(val_all.at[0], RHS)

    def apply(high, low, vectors):
        both = split(vectors)
        return join(dot(both, high[...]) + dot(both, low[...]))

    local = apply(factor_hi, factor_lo, scaled)

    copies[1].wait()
    values = coarse_in[...]
    top = values.astype(BF16)
    coarse_split[...] = jnp.zeros(coarse_split.shape, BF16)
    coarse_split[:coarse_rows, :] = top
    coarse_split[half : half + coarse_rows, :] = (values - top.astype(F32)).astype(BF16)
    arrive(idx_all, IDX)
    chunk = 256
    chunks = coarse_all // chunk
    small = lax.broadcasted_iota(jnp.int32, (chunk, 2 * wide), 0).astype(F32).astype(BF16)

    def one_column(s, carry):
        wanted = jnp.concatenate(
            [jnp.maximum(idx_all[4 * s + i], idx_all[4 * s + i + 1]) for i in (0, 2)], axis=1
        )

        def one_chunk(k, acc):
            start_at = k * chunk
            offset = wanted - start_at
            inside = jnp.logical_and(offset >= 0, offset < chunk)
            offset = jnp.where(inside, offset, -1).astype(F32).astype(BF16)
            picks = jnp.where(small == offset, jnp.ones_like(small), jnp.zeros_like(small))
            return acc + dot(coarse_split[:, pl.ds(start_at, chunk)], picks)

        acc = jnp.zeros((wide, 2 * wide), F32)
        if chunks <= 8:
            for k in range(chunks):
                acc = one_chunk(k, acc)
        else:
            acc = lax.fori_loop(
                0, chunks, lambda k, acc: one_chunk(pl.multiple_of(k, 1), acc), acc
            )
        values = join(acc)
        top = values.astype(BF16)
        at = pl.ds(pl.multiple_of(s * 2 * wide, 2 * wide), 2 * wide)
        columns[:half, at] = top
        columns[half:, at] = (values - top.astype(F32)).astype(BF16)
        return carry

    lax.fori_loop(0, count // 4, one_column, 0)

    def gathered(buffer):
        return split(
            jnp.concatenate([unpack(buffer[s], buffer[s + 1]) for s in range(0, count, 2)], axis=1)
        )

    arrive(val_all.at[0], RHS)
    solved = join(dot_nt(gathered(val_all.at[0]), columns[...]))
    solved = solved + pltpu.roll(solved, half, 1)
    val_all[1, me] = pack(solved)
    start(val_all.at[1], SOL)

    copies[2].wait()
    split_matrix(schur_in, schur_hi, schur_lo)

    at = lax.broadcasted_iota(jnp.int32, (wide, wide), 0)
    upper = (at >= half).astype(jnp.int32)
    number = upper * coarse_rows + at - upper * half
    number = jnp.where(at - upper * half < coarse_rows, number, -2 * coarse_all)

    def one_pick(s, carry):
        coarse_hot[pl.ds(pl.multiple_of(s * wide, wide), wide), :] = one_hot(
            number, own_coarse - s * 2 * coarse_rows
        )
        return carry

    lax.fori_loop(0, count // 2, one_pick, 0)

    for turn in range(2, MOST_SWEEPS + 1):
        inner = scaled - apply(schur_hi, schur_lo, local)
        later = local + apply(factor_hi, factor_lo, inner)
        more = jnp.broadcast_to(elements[...], local.shape) >= turn * ELEM_BASE
        local = jnp.where(more, later, local)

    arrive(val_all.at[1], SOL)
    read = join(dot(gathered(val_all.at[1]), coarse_hot[...]))
    correction = join(dot_nt(split(read), local_hot[...]))
    halved = weights * (local + correction)
    face_fill(1, halved)
    face_start(1)

    def lane_sum(values):
        return jnp.sum(values, axis=1, keepdims=True)

    rz = lane_sum(right_side * halved)
    precond = face_finish(1, halved)
    image = apply(schur_hi, schur_lo, precond)
    pq = lane_sum(precond * image)
    sum_lane = lax.broadcasted_iota(jnp.int32, (rhs, 128), 1)
    sum_case = lax.broadcasted_iota(jnp.int32, (rhs, 128), 0)
    upper_lane, lower_lane = sum_lane == sum_case + rhs, sum_lane == sum_case
    laid = jnp.where(lower_lane, rz, 0.0) + jnp.where(upper_lane, pq, 0.0)
    sum_all[me] = jnp.sum(laid, axis=0, keepdims=True)
    start(sum_all, SUM)
    face_fill(2, image)
    face_start(2)
    direction[...] = precond
    loads_out[...] = right_side
    image_out[...] = face_finish(2, image)
    arrive(sum_all, SUM)
    sums = sum_all[0]
    for i in range(1, count):
        sums = sums + sum_all[i]
    sums = jnp.broadcast_to(sums, (rhs, 128))
    alpha = lane_sum(jnp.where(lower_lane, sums, 0.0)) / lane_sum(jnp.where(upper_lane, sums, 0.0))
    alpha_out[...] = jnp.broadcast_to(alpha, alpha_out.shape)

    for kind, buffer in enumerate([idx_all, val_all.at[0], val_all.at[1], sum_all]):
        each(lambda d: all_copy(buffer, kind, d).wait_send())
    for turn in range(3):
        for slot in range(4):
            @pl.when(can_send[slot])
            def _():
                face_copy(turn, slot).wait_send()


def up(n, to):
    return -(-n // to) * to


def body(
    n_row, n_col, loads, schur, factor, coarse_inverse, elements, west_map, south_map,
    prim_local, prim_coarse,
):
    vectors = loads[0, 0].T
    rhs, unknowns = vectors.shape
    face = unknowns // 4
    coarse_rows, coarse_all = coarse_inverse.shape
    nprim = prim_local.shape[2]
    wide = 2 * up(max(nprim, coarse_rows), 64)
    count = n_row * n_col
    vmem = pl.BlockSpec(memory_space=pltpu.VMEM)
    hbm = pl.BlockSpec(memory_space=pl.ANY)
    dma = pltpu.SemaphoreType.DMA
    out = jax.ShapeDtypeStruct(vectors.shape, F32)
    direction, image, right_side, alpha = pl.pallas_call(
        functools.partial(kernel, n_row, n_col),
        out_shape=(out, out, out, out),
        in_specs=[vmem, hbm, hbm, hbm, vmem, vmem, vmem, vmem, vmem],
        out_specs=(vmem, vmem, vmem, vmem),
        scratch_shapes=[
            pltpu.VMEM((unknowns, unknowns), F32),
            pltpu.VMEM((unknowns, unknowns), F32),
            pltpu.VMEM((coarse_rows, coarse_all), F32),
            pltpu.VMEM((unknowns, unknowns), BF16),
            pltpu.VMEM((unknowns, unknowns), BF16),
            pltpu.VMEM((unknowns, unknowns), BF16),
            pltpu.VMEM((unknowns, unknowns), BF16),
            pltpu.VMEM((wide, coarse_all), BF16),
            pltpu.VMEM((wide, count // 2 * wide), BF16),
            pltpu.VMEM((face, face), BF16),
            pltpu.VMEM((face, face), BF16),
            pltpu.VMEM((unknowns, wide), BF16),
            pltpu.VMEM((count // 2 * wide, wide), BF16),
            pltpu.VMEM((8, wide), jnp.int32),
            pltpu.VMEM((count, 1, wide), jnp.int32),
            pltpu.VMEM((2, count, rhs // 2, wide), F32),
            pltpu.VMEM((count, 1, 128), F32),
            pltpu.VMEM((3, 4, rhs, face), F32),
            pltpu.VMEM((3, 4, rhs, face), F32),
            dma((3,)),
            dma((3, 4)),
            dma((3, 4)),
            dma((4, count)),
            dma((4, count)),
        ],
        compiler_params=pltpu.CompilerParams(collective_id=0, has_side_effects=True),
    )(
        vectors, schur[0, 0], factor[0, 0], coarse_inverse, elements,
        west_map[0], south_map[0], prim_local[0], prim_coarse[0],
    )
    solution = alpha * direction
    residual = right_side - alpha * image
    return solution.T[None, None], residual.T[None, None]


def solution(mesh):
    placed = (
        P("row", "col", None, None),
        P("row", "col", None, None),
        P("row", "col", None, None),
        P(("row", "col"), None),
        P("row", "col"),
        P("row", "col", None),
        P("row", "col", None),
        P("row", "col", None),
        P("row", "col", None),
    )
    return jax.shard_map(
        functools.partial(body, mesh.shape["row"], mesh.shape["col"]),
        mesh=mesh,
        in_specs=placed,
        out_specs=(P("row", "col", None, None), P("row", "col", None, None)),
        check_vma=False,
    )
```
